32 devices in a mesh: depth: 4 (over x, core), tile: 8 (over z, y).
Axes of the slice: x: 2, y: 2, z: 4, core: 2. Of those that a mesh axis runs over, the one named last changes fastest.
Arguments:
- density: bfloat16 [64, 256, 1024], P('depth', 'tile'), may hold values from -6 to 6
- row_shift: int32 [64], P('depth'), may hold values from -6 to 6
- brick_order: int32 [4], replicated, may hold values from 0 to 3, as said below
- tf_gain: float32 [4], replicated, may hold values from 0.5 to 2
- tf_bias: float32 [4], replicated, may hold values from -1 to 1
- light_dir: float32 [3], replicated, may hold values from -1 to 1
- background: float32 [3], replicated, may hold values from 0 to 1
Outputs:
- picture: float32 [4, 256, 1024], P(None, 'tile')
The draws below stay inside these ranges and needn't reach their ends.
Inputs may be any that keep to these rules, and one draw needn't show every extreme that they name: brick_order is a permutation in which, for every bit level l, bit l of brick_order[i] is bit l of i XOR a value that depends only on the bits of i above l.
All inputs are finite; a program needn't handle non-finite values.
Results may differ from the reference program's by a relative error of at most 0.0003.
Values may be sent and summed in bfloat16 or wider, within the bound.
A program may use at most 64 MiB of HBM per device.

```python
import jax
import jax.numpy as jnp
from jax import lax

W = 1024
SL_DEV = 16
MAXS = 6
NZ = 64
H = 256
N_DEPTH = 4


def shear_helper(key):
    folded = jax.random.fold_in(key, 7)
    keys = jax.random.split(folded, 4)
    level_count = N_DEPTH.bit_length() - 1
    flips = jax.random.randint(keys[0], (level_count, N_DEPTH), 0, 2)
    index = jnp.arange(N_DEPTH, dtype=jnp.int32)
    order = jnp.zeros((N_DEPTH,), jnp.int32)
    for level in range(level_count):
        prefix = jnp.right_shift(index, level + 1)
        own_bit = jnp.bitwise_and(jnp.right_shift(index, level), 1)
        new_bit = jnp.bitwise_xor(own_bit, flips[level][prefix])
        order = order + jnp.left_shift(new_bit, level)
    order = order.astype(jnp.int32)
    slope = jax.random.randint(keys[1], (), MAXS + 1, 2 * MAXS + 1)
    direction = 2 * jax.random.randint(keys[2], (), 0, 2) - 1
    jitter = jax.random.randint(keys[3], (NZ,), -1, 2)
    stored = jnp.arange(NZ, dtype=jnp.int32)
    position = order[stored // SL_DEV] * SL_DEV + stored % SL_DEV
    jitter = jnp.where((position == 0) | (position == NZ - 1), 0, jitter)
    base_shift = slope * (2 * position + 1 - NZ) // NZ
    shifts = jnp.clip(direction * (base_shift + jitter), -MAXS, MAXS).astype(jnp.int32)
    return (order, shifts)


def draw_brick_order(key, part):
    return shear_helper(key)[0]


def draw_row_shift(key, part):
    return shear_helper(key)[1]


def draw_density(key, part):
    folded = jax.random.fold_in(key, 3)
    first_key, second_key = jax.random.split(folded)
    base_field = jax.random.truncated_normal(first_key, -4.0, 4.0, (1, H, W), jnp.float32)
    noise_field = 0.5 * jax.random.truncated_normal(second_key, -4.0, 4.0, (NZ, H, W), jnp.float32)
    return (base_field + noise_field).astype(jnp.bfloat16)


def setup_inputs(seed: int = 0) -> dict:
    seeds = jax.random.split(jax.random.key(seed), 8)
    return {
        "density": draw_density(jax.random.fold_in(seeds[7], 71), 0),
        "row_shift": draw_row_shift(jax.random.fold_in(seeds[7], 71), 0),
        "brick_order": draw_brick_order(jax.random.fold_in(seeds[7], 71), 0),
        "tf_gain": jnp.clip(jax.random.uniform(seeds[3], (4,), jnp.float32, 0.5, 2.0), 0.5, 2.0),
        "tf_bias": jnp.clip(jax.random.uniform(seeds[4], (4,), jnp.float32, -1.0, 1.0), -1.0, 1.0),
        "light_dir": jnp.clip(jax.random.uniform(seeds[5], (3,), jnp.float32, -1.0, 1.0), -1.0, 1.0),
        "background": jnp.clip(jax.random.uniform(seeds[6], (3,), jnp.float32, 0.0, 1.0), 0.0, 1.0),
    }


optical_scale = 1.0

def reference(density, row_shift, brick_order, tf_gain, tf_bias, light_dir, background):
    total_slices = density.shape[0]
    height = density.shape[1]
    col_count = density.shape[2]
    rim_rows = MAXS + 1
    inverse = jnp.zeros((N_DEPTH,), jnp.int32).at[brick_order].set(jnp.arange(N_DEPTH, dtype=jnp.int32))

    def advance(carry, position):
        colour_sum, through = carry
        stored = (inverse[position // SL_DEV] * SL_DEV + position % SL_DEV).astype(jnp.int32)
        sheet = lax.dynamic_index_in_dim(density, stored, 0, keepdims=False)
        sheet = jnp.pad(sheet, ((rim_rows, rim_rows), (0, 0)))
        offset = (rim_rows - 1 - row_shift[stored]).astype(jnp.int32)
        sampled = lax.dynamic_slice_in_dim(sheet, offset, height + 2, 0).astype(jnp.float32)
        value = sampled[1:-1]
        grad_rows = 0.5 * (sampled[2:] - sampled[:-2])
        col_padded = jnp.pad(value, ((0, 0), (1, 1)))
        grad_cols = 0.5 * (col_padded[:, 2:] - col_padded[:, :-2])
        inverse_norm = lax.rsqrt(1.0 + grad_cols * grad_cols + grad_rows * grad_rows)
        shading = 0.25 + jnp.abs(light_dir[2] - light_dir[0] * grad_cols - light_dir[1] * grad_rows) * inverse_norm
        optical = jax.nn.softplus(tf_gain[3] * value + tf_bias[3]) * (optical_scale / total_slices)
        passed = jnp.exp(-optical)
        weight = through * (1.0 - passed)
        colours = jnp.stack([jax.nn.sigmoid(tf_gain[k] * value + tf_bias[k]) * shading for k in range(3)], 0)
        colour_sum = colour_sum + weight[None] * colours
        through = through * passed
        return ((colour_sum, through), None)
    start_carry = (jnp.zeros((3, height, col_count), jnp.float32), jnp.ones((height, col_count), jnp.float32))
    (colour_sum, through), _ = lax.scan(advance, start_carry, jnp.arange(total_slices, dtype=jnp.int32))
    colour = colour_sum + through[None] * background[:, None, None]
    return jnp.concatenate([colour, (1.0 - through)[None]], 0)
```

```python
import functools
import math

import jax
import jax.numpy as jnp
from jax import lax
from jax.experimental import pallas as pl
from jax.experimental.pallas import tpu as pltpu
from jax.sharding import PartitionSpec as P

LANES = 128
RIM = 8
MESH = pl.DeviceIdType.MESH


def kernel(
    sizes,
    density,
    row_shift,
    brick_order,
    gain,
    bias,
    light,
    background,
    out,
    ext,
    bundle,
    near,
    far,
    part,
    got,
    comp,
    halo_sems,
    swap_sems,
):
    n_depth, n_tile, halo_chunks = sizes
    slices, rows, cols = density.shape
    levels = n_depth.bit_length() - 1
    blocks = rows // RIM
    half = cols // 2
    half_tiles = half // LANES
    col_tiles = cols // LANES
    total = slices * n_depth
    me_d = lax.axis_index("depth")
    me_t = lax.axis_index("tile")
    odd = lax.rem(me_t, 2)
    pair_t = me_t + 1 - 2 * odd
    low_ok = me_t >= 2
    high_ok = me_t + 2 < n_tile
    is_odd = odd == 1
    sends_on = jnp.logical_or(
        jnp.logical_and(is_odd, low_ok), jnp.logical_and(jnp.logical_not(is_odd), high_ok)
    )
    gets_far = jnp.logical_or(
        jnp.logical_and(is_odd, high_ok), jnp.logical_and(jnp.logical_not(is_odd), low_ok)
    )
    on_t = me_t + 2 - 4 * odd

    def flip(level):
        bit = lax.rem(me_d // (2**level), 2)
        return me_d + (1 - 2 * bit) * 2**level

    barrier = pltpu.get_barrier_semaphore()
    pl.semaphore_signal(barrier, inc=1, device_id={"tile": pair_t}, device_id_type=MESH)
    for level in range(levels):
        pl.semaphore_signal(barrier, inc=1, device_id={"depth": flip(level)}, device_id_type=MESH)

    @pl.when(low_ok)
    def _():
        pl.semaphore_signal(barrier, inc=1, device_id={"tile": me_t - 2}, device_id_type=MESH)

    @pl.when(high_ok)
    def _():
        pl.semaphore_signal(barrier, inc=1, device_id={"tile": me_t + 2}, device_id_type=MESH)

    place = lax.broadcasted_iota(jnp.int32, (RIM, cols), 0)

    def build(g, _):
        picked = []
        for i in range(2):
            j = 2 * g + i
            shift = row_shift[j]
            first = density[j, 0:16, :].astype(jnp.float32)[0:RIM]
            last = density[j, rows - 16 : rows, :].astype(jnp.float32)[16 - RIM :]
            use_last = jnp.where(shift > 0, 0, jnp.where(shift < 0, RIM, RIM // 2))
            picked.append(jnp.where(place >= use_last, last, first))
        bundle[g] = jnp.concatenate(picked, 0).astype(bundle.dtype)
        return 0

    lax.fori_loop(0, slices // 2, build, 0)

    peers = 1 + levels + low_ok.astype(jnp.int32) + high_ok.astype(jnp.int32)
    pl.semaphore_wait(barrier, peers)

    per = slices // 2 // halo_chunks
    near_copies = []
    far_copies = []
    for c in range(halo_chunks):
        span = pl.ds(c * per, per)
        near_copies.append(
            pltpu.make_async_remote_copy(
                src_ref=bundle.at[span],
                dst_ref=near.at[span],
                send_sem=halo_sems.at[0, c],
                recv_sem=halo_sems.at[1, c],
                device_id={"tile": pair_t},
                device_id_type=MESH,
            )
        )
        far_copies.append(
            pltpu.make_async_remote_copy(
                src_ref=near.at[span],
                dst_ref=far.at[span],
                send_sem=halo_sems.at[2, c],
                recv_sem=halo_sems.at[3, c],
                device_id={"tile": on_t},
                device_id_type=MESH,
            )
        )
        near_copies[-1].start()

    @pl.when(jnp.logical_not(gets_far))
    def _():
        far[...] = jnp.zeros_like(far)

    def fill(j, _):
        sheet = density[j].astype(jnp.float32)
        for t in range(col_tiles):
            ext[j, t, RIM : RIM + rows, :] = sheet[:, t * LANES : (t + 1) * LANES]
        return 0

    lax.fori_loop(0, slices, fill, 0)

    def pass_on(c):
        near_copies[c].wait_recv()

        @pl.when(sends_on)
        def _():
            far_copies[c].start()

    lane = lax.broadcasted_iota(jnp.int32, (RIM, LANES), 1)
    is_first = lane == 0
    is_last = lane == LANES - 1
    log2e = math.log2(math.e)
    half_gain = [0.5 * gain[k] for k in range(3)]
    half_bias = [0.5 * bias[k] for k in range(3)]
    opt_gain = gain[3] * log2e
    opt_bias = bias[3] * log2e
    light_c = 0.5 * light[0]
    light_r = 0.5 * light[1]
    light_z = light[2]

    def render(block, side):
        def step(j, carry):
            base = RIM + block * RIM - 1 - row_shift[j]
            tiles = range(side * half_tiles - 1, (side + 1) * half_tiles + 1)
            value = [
                ext[j, t, pl.ds(base + 1, RIM), :] if 0 <= t < col_tiles else None for t in tiles
            ]
            zero = jnp.zeros((RIM, LANES), jnp.float32)
            value = [zero if v is None else v for v in value]
            new = []
            for i in range(half_tiles):
                t = side * half_tiles + i
                through, base_sum, c0, c1, c2 = carry[i]
                v = value[i + 1]
                above = ext[j, t, pl.ds(base, RIM), :]
                below = ext[j, t, pl.ds(base + 2, RIM), :]
                left = pltpu.roll(jnp.where(is_last, value[i], v), 1, 1)
                right = pltpu.roll(jnp.where(is_first, value[i + 2], v), LANES - 1, 1)
                drow = below - above
                dcol = right - left
                norm = lax.rsqrt(4.0 + (dcol * dcol + drow * drow))
                shade = 0.125 + jnp.abs(light_z - light_c * dcol - light_r * drow) * norm
                grow = jnp.exp2(opt_gain * v + opt_bias)
                passed = jnp.exp2(jnp.log(1.0 + grow) * (-log2e / total))
                after = through * passed
                weight = (through - after) * shade
                sums = [
                    c + weight * jnp.tanh(half_gain[k] * v + half_bias[k])
                    for k, c in enumerate((c0, c1, c2))
                ]
                new.append((after, base_sum + weight, *sums))
            return tuple(new)

        zero = jnp.zeros((RIM, LANES), jnp.float32)
        one = jnp.ones((RIM, LANES), jnp.float32)
        start = tuple((one, zero, zero, zero, zero) for _ in range(half_tiles))
        done = lax.fori_loop(0, slices, step, start)
        for i in range(half_tiles):
            through, base_sum, *sums = done[i]
            at = slice(i * LANES, (i + 1) * LANES)
            for k in range(3):
                part[block, side, k, :, at] = base_sum + sums[k]
            part[block, side, 3, :, at] = through

    side_bit = lax.rem(me_d, 2)
    position = brick_order[me_d]

    def swap(level, block):
        if level == 0:
            source = part.at[block, 1 - side_bit]
        else:
            source = comp.at[level - 1, block]
        return pltpu.make_async_remote_copy(
            src_ref=source,
            dst_ref=got.at[level, block],
            send_sem=swap_sems.at[0, level, block],
            recv_sem=swap_sems.at[1, level, block],
            device_id={"depth": flip(level if level < levels else 0)},
            device_id_type=MESH,
        )

    def merge(level, block):
        swap(level, block).wait_recv()
        mine = part[block, side_bit] if level == 0 else comp[level - 1, block]
        theirs = got[level, block]
        front = lax.rem(position // (2**level), 2) == 0
        near_part = jnp.where(front, mine, theirs)
        far_part = jnp.where(front, theirs, mine)
        through = near_part[3]
        colour = [near_part[k] + through * far_part[k] for k in range(3)]
        through = through * far_part[3]
        if level == levels - 1:
            colour = [colour[k] + through * background[k] for k in range(3)]
            through = 1.0 - through
        for k in range(3):
            comp[level, block, k] = colour[k]
        comp[level, block, 3] = through
        swap(level + 1, block).start()

    inner = list(range(1, blocks - 1))
    order = inner + [0, blocks - 1]
    pending = []
    passed_on = 0
    for n, block in enumerate(inner):
        for side in range(2):
            render(block, side)
            if passed_on < halo_chunks:
                pass_on(passed_on)
                passed_on += 1
        swap(0, block).start()
        pending.append(block)
        if len(pending) > 1:
            merge(0, pending.pop(0))
    for c in range(passed_on, halo_chunks):
        pass_on(c)

    for c in range(halo_chunks):

        @pl.when(gets_far)
        def _():
            far_copies[c].wait_recv()

        def fill_rim(g, _):
            near_rows = near[g].astype(jnp.float32)
            far_rows = far[g].astype(jnp.float32)
            above = jnp.where(is_odd, near_rows, far_rows)
            below = jnp.where(is_odd, far_rows, near_rows)
            for i in range(2):
                for t in range(col_tiles):
                    at = slice(t * LANES, (t + 1) * LANES)
                    rim = slice(i * RIM, (i + 1) * RIM)
                    ext[2 * g + i, t, 0:RIM, :] = above[rim, at]
                    ext[2 * g + i, t, RIM + rows : 2 * RIM + rows, :] = below[rim, at]
            return 0

        lax.fori_loop(c * per, (c + 1) * per, fill_rim, 0)

    for block in order[len(inner) :]:
        for side in range(2):
            render(block, side)
        swap(0, block).start()
        pending.append(block)
        merge(0, pending.pop(0))
    for block in pending:
        merge(0, block)
    for level in range(1, levels):
        for block in order:
            merge(level, block)
    for block in order:
        swap(levels, block).wait_recv()
        at = pl.ds(block * RIM, RIM)
        mine = comp[levels - 1, block]
        theirs = got[levels, block]
        upper = side_bit == 1
        out[:, at, 0:half] = jnp.where(upper, theirs, mine)
        out[:, at, half:cols] = jnp.where(upper, mine, theirs)

    for c in range(halo_chunks):
        near_copies[c].wait_send()

        @pl.when(sends_on)
        def _():
            far_copies[c].wait_send()

    for level in range(levels + 1):
        for block in order:
            swap(level, block).wait_send()


def on_device(
    density, row_shift, brick_order, tf_gain, tf_bias, light_dir, background, *, n_depth, n_tile
):
    slices, rows, cols = density.shape
    levels = n_depth.bit_length() - 1
    blocks = rows // RIM
    halo_chunks = 4
    smem = pl.BlockSpec(memory_space=pltpu.SMEM)
    vmem = pl.BlockSpec(memory_space=pltpu.VMEM)
    halo = pltpu.VMEM((slices // 2, 2 * RIM, cols), density.dtype)
    image = (4, RIM, cols // 2)
    return pl.pallas_call(
        functools.partial(kernel, (n_depth, n_tile, halo_chunks)),
        out_shape=jax.ShapeDtypeStruct((4, rows, cols), jnp.float32),
        in_specs=[vmem] + [smem] * 6,
        out_specs=vmem,
        scratch_shapes=[
            pltpu.VMEM((slices, cols // LANES, rows + 2 * RIM, LANES), jnp.float32),
            halo,
            halo,
            halo,
            pltpu.VMEM((blocks, 2) + image, jnp.float32),
            pltpu.VMEM((levels + 1, blocks) + image, jnp.float32),
            pltpu.VMEM((levels, blocks) + image, jnp.float32),
            pltpu.SemaphoreType.DMA((4, halo_chunks)),
            pltpu.SemaphoreType.DMA((2, levels + 1, blocks)),
        ],
        compiler_params=pltpu.CompilerParams(collective_id=0, has_side_effects=True),
    )(density, row_shift, brick_order, tf_gain, tf_bias, light_dir, background)


def solution(mesh):
    placed = (P("depth", "tile", None), P("depth"), P(), P(), P(), P(), P())
    body = functools.partial(
        on_device, n_depth=mesh.shape["depth"], n_tile=mesh.shape["tile"]
    )
    return jax.shard_map(
        body, mesh=mesh, in_specs=placed, out_specs=P(None, "tile", None), check_vma=False
    )
```

```python
import functools
import math

import jax
import jax.numpy as jnp
from jax import lax
from jax.experimental import pallas as pl
from jax.experimental.pallas import tpu as pltpu
from jax.sharding import PartitionSpec as P

LANES = 128
RIM = 8
MESH = pl.DeviceIdType.MESH


def kernel(
    sizes,
    stored,
    row_shift_arg,
    brick_order_arg,
    gain_arg,
    bias_arg,
    light_arg,
    background_arg,
    out,
    row_shift,
    brick_order,
    gain,
    bias,
    light,
    background,
    density,
    state,
    ext,
    bundle,
    near,
    far,
    part,
    got,
    comp,
    load_sems,
    small_sems,
    halo_sems,
    swap_sems,
):
    n_depth, n_tile, halo_chunks = sizes
    slices, rows, cols = density.shape
    levels = n_depth.bit_length() - 1
    blocks = rows // RIM
    half = cols // 2
    half_tiles = half // LANES
    col_tiles = cols // LANES
    total = slices * n_depth
    me_d = lax.axis_index("depth")
    me_t = lax.axis_index("tile")
    odd = lax.rem(me_t, 2)
    pair_t = me_t + 1 - 2 * odd
    low_ok = me_t >= 2
    high_ok = me_t + 2 < n_tile
    is_odd = odd == 1
    sends_on = jnp.logical_or(
        jnp.logical_and(is_odd, low_ok), jnp.logical_and(jnp.logical_not(is_odd), high_ok)
    )
    gets_far = jnp.logical_or(
        jnp.logical_and(is_odd, high_ok), jnp.logical_and(jnp.logical_not(is_odd), low_ok)
    )
    on_t = me_t + 2 - 4 * odd

    def flip(level):
        bit = lax.rem(me_d // (2**level), 2)
        return me_d + (1 - 2 * bit) * 2**level

    loads = [
        pltpu.make_async_copy(
            stored.at[:, pl.ds(at, size)], density.at[:, pl.ds(at, size)], load_sems.at[i]
        )
        for i, (at, size) in enumerate(
            [(0, RIM), (rows - RIM, RIM), (RIM, rows - 2 * RIM)]
        )
    ]
    small = [
        pltpu.make_async_copy(arg, held, small_sems.at[i])
        for i, (arg, held) in enumerate(
            [
                (row_shift_arg, row_shift),
                (brick_order_arg, brick_order),
                (gain_arg, gain),
                (bias_arg, bias),
                (light_arg, light),
                (background_arg, background),
            ]
        )
    ]
    for load in small + loads:
        load.start()

    barrier = pltpu.get_barrier_semaphore()
    pl.semaphore_signal(barrier, inc=1, device_id={"tile": pair_t}, device_id_type=MESH)
    for level in range(levels):
        pl.semaphore_signal(barrier, inc=1, device_id={"depth": flip(level)}, device_id_type=MESH)

    @pl.when(low_ok)
    def _():
        pl.semaphore_signal(barrier, inc=1, device_id={"tile": me_t - 2}, device_id_type=MESH)

    @pl.when(high_ok)
    def _():
        pl.semaphore_signal(barrier, inc=1, device_id={"tile": me_t + 2}, device_id_type=MESH)

    place = lax.broadcasted_iota(jnp.int32, (RIM, cols), 0)

    def build(g, _):
        picked = []
        for i in range(2):
            j = 2 * g + i
            shift = row_shift[j]
            first = density[j, 0:RIM, :].astype(jnp.float32)
            last = density[j, rows - RIM : rows, :].astype(jnp.float32)
            use_last = jnp.where(shift > 0, 0, jnp.where(shift < 0, RIM, RIM // 2))
            picked.append(jnp.where(place >= use_last, last, first))
        bundle[g] = jnp.concatenate(picked, 0).astype(bundle.dtype)
        return 0

    for load in small + loads[:2]:
        load.wait()
    lax.fori_loop(0, slices // 2, build, 0)

    peers = 1 + levels + low_ok.astype(jnp.int32) + high_ok.astype(jnp.int32)
    pl.semaphore_wait(barrier, peers)

    per = slices // 2 // halo_chunks
    near_copies = []
    far_copies = []
    for c in range(halo_chunks):
        span = pl.ds(c * per, per)
        near_copies.append(
            pltpu.make_async_remote_copy(
                src_ref=bundle.at[span],
                dst_ref=near.at[span],
                send_sem=halo_sems.at[0, c],
                recv_sem=halo_sems.at[1, c],
                device_id={"tile": pair_t},
                device_id_type=MESH,
            )
        )
        far_copies.append(
            pltpu.make_async_remote_copy(
                src_ref=near.at[span],
                dst_ref=far.at[span],
                send_sem=halo_sems.at[2, c],
                recv_sem=halo_sems.at[3, c],
                device_id={"tile": on_t},
                device_id_type=MESH,
            )
        )
        near_copies[-1].start()

    @pl.when(jnp.logical_not(gets_far))
    def _():
        far[...] = jnp.zeros_like(far)

    loads[2].wait()

    def fill(j, _):
        sheet = density[j].astype(jnp.float32)
        ext[j, 0] = jnp.zeros((rows + 2 * RIM, LANES), jnp.float32)
        ext[j, col_tiles + 1] = jnp.zeros((rows + 2 * RIM, LANES), jnp.float32)
        for t in range(col_tiles):
            ext[j, t + 1, RIM : RIM + rows, :] = sheet[:, t * LANES : (t + 1) * LANES]
        return 0

    lax.fori_loop(0, slices, fill, 0)

    def pass_on(c):
        near_copies[c].wait_recv()

        @pl.when(sends_on)
        def _():
            far_copies[c].start()

    lane = lax.broadcasted_iota(jnp.int32, (RIM, LANES), 1)
    is_first = lane == 0
    is_last = lane == LANES - 1
    log2e = math.log2(math.e)
    half_gain = [0.5 * gain[k] for k in range(3)]
    half_bias = [0.5 * bias[k] for k in range(3)]
    opt_gain = gain[3] * log2e
    opt_bias = bias[3] * log2e
    light_c = 0.5 * light[0]
    light_r = 0.5 * light[1]
    light_z = light[2]

    def advance(block, side, low, high, carry):
        def step(j, carry):
            base = RIM + block * RIM - 1 - row_shift[j]
            first_tile = side * half_tiles
            value = [ext[j, first_tile + i, pl.ds(base + 1, RIM), :] for i in range(half_tiles + 2)]
            new = []
            for i in range(half_tiles):
                t = first_tile + i + 1
                through, base_sum, c0, c1, c2 = carry[i]
                v = value[i + 1]
                above = ext[j, t, pl.ds(base, RIM), :]
                below = ext[j, t, pl.ds(base + 2, RIM), :]
                left = pltpu.roll(jnp.where(is_last, value[i], v), 1, 1)
                right = pltpu.roll(jnp.where(is_first, value[i + 2], v), LANES - 1, 1)
                drow = below - above
                dcol = right - left
                norm = lax.rsqrt(4.0 + (dcol * dcol + drow * drow))
                shade = 0.125 + jnp.abs(light_z - light_c * dcol - light_r * drow) * norm
                grow = jnp.exp2(opt_gain * v + opt_bias)
                passed = jnp.exp2(jnp.log(1.0 + grow) * (-log2e / total))
                after = through * passed
                weight = (through - after) * shade
                sums = [
                    c + weight * jnp.tanh(half_gain[k] * v + half_bias[k])
                    for k, c in enumerate((c0, c1, c2))
                ]
                new.append((after, base_sum + weight, *sums))
            return tuple(new)

        return lax.fori_loop(low, high, step, carry, unroll=4)

    def finish(block, side, carry):
        for i in range(half_tiles):
            through, base_sum, *sums = carry[i]
            at = slice(i * LANES, (i + 1) * LANES)
            for k in range(3):
                part[block, side, k, :, at] = base_sum + sums[k]
            part[block, side, 3, :, at] = through

    zero = jnp.zeros((RIM, LANES), jnp.float32)
    one = jnp.ones((RIM, LANES), jnp.float32)
    start = tuple((one, zero, zero, zero, zero) for _ in range(half_tiles))

    def render(block):
        def one_side(side, _):
            finish(block, side, advance(block, side, 0, slices, start))
            return 0

        lax.fori_loop(0, 2, one_side, 0)

    def render_rim(c):
        def one_piece(piece, _):
            rim = piece // 2
            side = lax.rem(piece, 2)
            block = rim * (blocks - 1)
            if c == 0:
                carry = start
            else:
                carry = tuple(
                    tuple(state[piece, i, k] for k in range(5)) for i in range(half_tiles)
                )
            carry = advance(block, side, c * per * 2, (c + 1) * per * 2, carry)
            if c == halo_chunks - 1:
                finish(block, side, carry)
            else:
                for i in range(half_tiles):
                    for k in range(5):
                        state[piece, i, k] = carry[i][k]
            return 0

        lax.fori_loop(0, 4, one_piece, 0)

    side_bit = lax.rem(me_d, 2)
    position = brick_order[me_d]

    def swap(level, block):
        if level == 0:
            source = part.at[block, 1 - side_bit]
        else:
            source = comp.at[level - 1, block]
        return pltpu.make_async_remote_copy(
            src_ref=source,
            dst_ref=got.at[level, block],
            send_sem=swap_sems.at[0, level, block],
            recv_sem=swap_sems.at[1, level, block],
            device_id={"depth": flip(level if level < levels else 0)},
            device_id_type=MESH,
        )

    def merge(level, block):
        swap(level, block).wait_recv()
        mine = part[block, side_bit] if level == 0 else comp[level - 1, block]
        theirs = got[level, block]
        front = lax.rem(position // (2**level), 2) == 0
        near_part = jnp.where(front, mine, theirs)
        far_part = jnp.where(front, theirs, mine)
        through = near_part[3]
        colour = [near_part[k] + through * far_part[k] for k in range(3)]
        through = through * far_part[3]
        if level == levels - 1:
            colour = [0.5 * (colour[k] + through * background[k]) for k in range(3)]
            through = 0.5 - 0.5 * through
        for k in range(3):
            comp[level, block, k] = colour[k]
        comp[level, block, 3] = through
        swap(level + 1, block).start()

    inner = list(range(1, blocks - 1))
    order = inner + [0, blocks - 1]
    passed_on = 0
    for n, block in enumerate(inner):
        render(block)
        swap(0, block).start()
        if n > 0:
            merge(0, inner[n - 1])
        if passed_on < halo_chunks - 1:
            pass_on(passed_on)
            passed_on += 1
    merge(0, inner[-1])

    for c in range(halo_chunks):
        if c + 1 >= passed_on and passed_on < halo_chunks:
            pass_on(passed_on)
            passed_on += 1

        @pl.when(gets_far)
        def _():
            far_copies[c].wait_recv()

        def fill_rim(g, _):
            near_rows = near[g].astype(jnp.float32)
            far_rows = far[g].astype(jnp.float32)
            above = jnp.where(is_odd, near_rows, far_rows)
            below = jnp.where(is_odd, far_rows, near_rows)
            for i in range(2):
                for t in range(col_tiles):
                    at = slice(t * LANES, (t + 1) * LANES)
                    rim = slice(i * RIM, (i + 1) * RIM)
                    ext[2 * g + i, t + 1, 0:RIM, :] = above[rim, at]
                    ext[2 * g + i, t + 1, RIM + rows : 2 * RIM + rows, :] = below[rim, at]
            return 0

        lax.fori_loop(c * per, (c + 1) * per, fill_rim, 0)
        render_rim(c)

    outer = [0, blocks - 1]
    for block in outer:
        swap(0, block).start()
    for level in range(1, levels):
        for block in inner:
            merge(level, block)
    for level in range(levels):
        for block in outer:
            merge(level, block)
    for block in order:
        swap(levels, block).wait_recv()
        at = pl.ds(block * RIM, RIM)
        mine = comp[levels - 1, block]
        theirs = got[levels, block]
        upper = side_bit == 1
        out[:, at, 0:half] = jnp.where(upper, theirs, mine)
        out[:, at, half:cols] = jnp.where(upper, mine, theirs)

    for c in range(halo_chunks):
        near_copies[c].wait_send()

        @pl.when(sends_on)
        def _():
            far_copies[c].wait_send()

    for level in range(levels + 1):
        for block in order:
            swap(level, block).wait_send()


def on_device(
    density, row_shift, brick_order, tf_gain, tf_bias, light_dir, background, *, n_depth, n_tile
):
    slices, rows, cols = density.shape
    levels = n_depth.bit_length() - 1
    blocks = rows // RIM
    halo_chunks = 4
    vmem = pl.BlockSpec(memory_space=pltpu.VMEM)
    halo = pltpu.VMEM((slices // 2, 2 * RIM, cols), density.dtype)
    image = (4, RIM, cols // 2)
    small_args = (row_shift, brick_order, tf_gain, tf_bias, light_dir, background)
    scaled = pl.pallas_call(
        functools.partial(kernel, (n_depth, n_tile, halo_chunks)),
        out_shape=jax.ShapeDtypeStruct((4, rows, cols), jnp.float32),
        in_specs=[pl.BlockSpec(memory_space=pltpu.HBM)] * 7,
        out_specs=vmem,
        scratch_shapes=[
            *[pltpu.SMEM(arg.shape, arg.dtype) for arg in small_args],
            pltpu.VMEM(density.shape, density.dtype),
            pltpu.VMEM((4, cols // 2 // LANES, 5, RIM, LANES), jnp.float32),
            pltpu.VMEM((slices, cols // LANES + 2, rows + 2 * RIM, LANES), jnp.float32),
            halo,
            halo,
            halo,
            pltpu.VMEM((blocks, 2) + image, jnp.float32),
            pltpu.VMEM((levels + 1, blocks) + image, jnp.float32),
            pltpu.VMEM((levels, blocks) + image, jnp.float32),
            pltpu.SemaphoreType.DMA((3,)),
            pltpu.SemaphoreType.DMA((len(small_args),)),
            pltpu.SemaphoreType.DMA((4, halo_chunks)),
            pltpu.SemaphoreType.DMA((2, levels + 1, blocks)),
        ],
        compiler_params=pltpu.CompilerParams(
            collective_id=0, has_side_effects=True, vmem_limit_bytes=20 * 2**20
        ),
    )(*[pltpu.with_memory_space_constraint(arg, pltpu.HBM) for arg in (density, *small_args)])
    return scaled + scaled


def solution(mesh):
    placed = (P("depth", "tile", None), P("depth"), P(), P(), P(), P(), P())
    body = functools.partial(
        on_device, n_depth=mesh.shape["depth"], n_tile=mesh.shape["tile"]
    )
    return jax.shard_map(
        body, mesh=mesh, in_specs=placed, out_specs=P(None, "tile", None), check_vma=False
    )
```

```python
import functools
import math

import jax
import jax.numpy as jnp
from jax import lax
from jax.experimental import pallas as pl
from jax.experimental.pallas import tpu as pltpu
from jax.sharding import PartitionSpec as P

LANES = 128
RIM = 8
MESH = pl.DeviceIdType.MESH


def kernel(
    sizes,
    stored,
    row_shift_arg,
    brick_order_arg,
    gain_arg,
    bias_arg,
    light_arg,
    background_arg,
    out,
    row_shift,
    brick_order,
    gain,
    bias,
    light,
    background,
    density,
    state,
    ext,
    bundle,
    near,
    far,
    part,
    got,
    comp,
    load_sems,
    small_sems,
    halo_sems,
    swap_sems,
):
    n_depth, n_tile, halo_chunks = sizes
    slices, rows, cols = density.shape
    levels = n_depth.bit_length() - 1
    blocks = rows // RIM
    half = cols // 2
    half_tiles = half // LANES
    col_tiles = cols // LANES
    total = slices * n_depth
    me_d = lax.axis_index("depth")
    me_t = lax.axis_index("tile")
    odd = lax.rem(me_t, 2)
    pair_t = me_t + 1 - 2 * odd
    low_ok = me_t >= 2
    high_ok = me_t + 2 < n_tile
    is_odd = odd == 1
    sends_on = jnp.logical_or(
        jnp.logical_and(is_odd, low_ok), jnp.logical_and(jnp.logical_not(is_odd), high_ok)
    )
    gets_far = jnp.logical_or(
        jnp.logical_and(is_odd, high_ok), jnp.logical_and(jnp.logical_not(is_odd), low_ok)
    )
    on_t = me_t + 2 - 4 * odd

    def flip(level):
        bit = lax.rem(me_d // (2**level), 2)
        return me_d + (1 - 2 * bit) * 2**level

    loads = [
        pltpu.make_async_copy(
            stored.at[:, pl.ds(at, size)], density.at[:, pl.ds(at, size)], load_sems.at[i]
        )
        for i, (at, size) in enumerate(
            [(0, RIM), (rows - RIM, RIM), (RIM, rows - 2 * RIM)]
        )
    ]
    small = [
        pltpu.make_async_copy(arg, held, small_sems.at[i])
        for i, (arg, held) in enumerate(
            [
                (row_shift_arg, row_shift),
                (brick_order_arg, brick_order),
                (gain_arg, gain),
                (bias_arg, bias),
                (light_arg, light),
                (background_arg, background),
            ]
        )
    ]
    for load in small + loads:
        load.start()

    barrier = pltpu.get_barrier_semaphore()
    pl.semaphore_signal(barrier, inc=1, device_id={"tile": pair_t}, device_id_type=MESH)
    for level in range(levels):
        pl.semaphore_signal(barrier, inc=1, device_id={"depth": flip(level)}, device_id_type=MESH)

    @pl.when(low_ok)
    def _():
        pl.semaphore_signal(barrier, inc=1, device_id={"tile": me_t - 2}, device_id_type=MESH)

    @pl.when(high_ok)
    def _():
        pl.semaphore_signal(barrier, inc=1, device_id={"tile": me_t + 2}, device_id_type=MESH)

    place = lax.broadcasted_iota(jnp.int32, (RIM, cols), 0)

    def build(g, _):
        picked = []
        for i in range(2):
            j = 2 * g + i
            shift = row_shift[j]
            first = density[j, 0:RIM, :].astype(jnp.float32)
            last = density[j, rows - RIM : rows, :].astype(jnp.float32)
            use_last = jnp.where(shift > 0, 0, jnp.where(shift < 0, RIM, RIM // 2))
            picked.append(jnp.where(place >= use_last, last, first))
        bundle[g] = jnp.concatenate(picked, 0).astype(bundle.dtype)
        return 0

    for load in small + loads[:2]:
        load.wait()
    lax.fori_loop(0, slices // 2, build, 0)

    peers = 1 + levels + low_ok.astype(jnp.int32) + high_ok.astype(jnp.int32)
    pl.semaphore_wait(barrier, peers)

    per = slices // 2 // halo_chunks
    near_copies = []
    far_copies = []
    for c in range(halo_chunks):
        span = pl.ds(c * per, per)
        near_copies.append(
            pltpu.make_async_remote_copy(
                src_ref=bundle.at[span],
                dst_ref=near.at[span],
                send_sem=halo_sems.at[0, c],
                recv_sem=halo_sems.at[1, c],
                device_id={"tile": pair_t},
                device_id_type=MESH,
            )
        )
        far_copies.append(
            pltpu.make_async_remote_copy(
                src_ref=near.at[span],
                dst_ref=far.at[span],
                send_sem=halo_sems.at[2, c],
                recv_sem=halo_sems.at[3, c],
                device_id={"tile": on_t},
                device_id_type=MESH,
            )
        )
        near_copies[-1].start()

    @pl.when(jnp.logical_not(gets_far))
    def _():
        far[...] = jnp.zeros_like(far)

    loads[2].wait()

    def fill(j, _):
        sheet = density[j].astype(jnp.float32)
        ext[j, 0] = jnp.zeros((rows + 2 * RIM, LANES), jnp.float32)
        ext[j, col_tiles + 1] = jnp.zeros((rows + 2 * RIM, LANES), jnp.float32)
        for t in range(col_tiles):
            ext[j, t + 1, RIM : RIM + rows, :] = sheet[:, t * LANES : (t + 1) * LANES]
        return 0

    lax.fori_loop(0, slices, fill, 0)

    def pass_on(c):
        near_copies[c].wait_recv()

        @pl.when(sends_on)
        def _():
            far_copies[c].start()

    lane = lax.broadcasted_iota(jnp.int32, (RIM, LANES), 1)
    is_first = lane == 0
    is_last = lane == LANES - 1
    log2e = math.log2(math.e)
    half_gain = [0.5 * gain[k] for k in range(3)]
    half_bias = [0.5 * bias[k] for k in range(3)]
    opt_gain = gain[3] * log2e
    opt_bias = bias[3] * log2e
    light_c = 0.5 * light[0]
    light_r = 0.5 * light[1]
    light_z = light[2]

    def advance(block, side, low, high, carry):
        def step(j, carry):
            base = RIM + block * RIM - 1 - row_shift[j]
            first_tile = side * half_tiles
            value = [ext[j, first_tile + i, pl.ds(base + 1, RIM), :] for i in range(half_tiles + 2)]
            new = []
            for i in range(half_tiles):
                t = first_tile + i + 1
                through, base_sum, c0, c1, c2 = carry[i]
                v = value[i + 1]
                above = ext[j, t, pl.ds(base, RIM), :]
                below = ext[j, t, pl.ds(base + 2, RIM), :]
                left = pltpu.roll(jnp.where(is_last, value[i], v), 1, 1)
                right = pltpu.roll(jnp.where(is_first, value[i + 2], v), LANES - 1, 1)
                drow = below - above
                dcol = right - left
                norm = lax.rsqrt(4.0 + (dcol * dcol + drow * drow))
                shade = 0.125 + jnp.abs(light_z - light_c * dcol - light_r * drow) * norm
                grow = jnp.exp2(opt_gain * v + opt_bias)
                passed = jnp.exp2(jnp.log(1.0 + grow) * (-log2e / total))
                after = through * passed
                weight = (through - after) * shade
                sums = [
                    c + weight * jnp.tanh(half_gain[k] * v + half_bias[k])
                    for k, c in enumerate((c0, c1, c2))
                ]
                new.append((after, base_sum + weight, *sums))
            return tuple(new)

        return lax.fori_loop(low, high, step, carry, unroll=min(4, high - low))

    def finish(block, side, carry):
        for i in range(half_tiles):
            through, base_sum, *sums = carry[i]
            at = slice(i * LANES, (i + 1) * LANES)
            for k in range(3):
                part[block, side, k, :, at] = base_sum + sums[k]
            part[block, side, 3, :, at] = through

    zero = jnp.zeros((RIM, LANES), jnp.float32)
    one = jnp.ones((RIM, LANES), jnp.float32)
    start = tuple((one, zero, zero, zero, zero) for _ in range(half_tiles))

    def render(block):
        def one_side(side, _):
            finish(block, side, advance(block, side, 0, slices, start))
            return 0

        lax.fori_loop(0, 2, one_side, 0)

    def render_rim(c):
        def one_piece(piece, block):
            side = lax.rem(piece, 2)
            if c == 0:
                carry = start
            else:
                carry = tuple(
                    tuple(state[piece, i, k] for k in range(5)) for i in range(half_tiles)
                )
            carry = advance(block, side, c * per * 2, (c + 1) * per * 2, carry)
            if c == halo_chunks - 1:
                finish(block, side, carry)
            else:
                for i in range(half_tiles):
                    for k in range(5):
                        state[piece, i, k] = carry[i][k]
            return block

        for rim, block in enumerate(outer):
            lax.fori_loop(2 * rim, 2 * rim + 2, one_piece, block)
            if c == halo_chunks - 1:
                swap(0, block).start()

    side_bit = lax.rem(me_d, 2)
    position = brick_order[me_d]

    def swap(level, block):
        if level == 0:
            source = part.at[block, 1 - side_bit]
        else:
            source = comp.at[level - 1, block]
        return pltpu.make_async_remote_copy(
            src_ref=source,
            dst_ref=got.at[level, block],
            send_sem=swap_sems.at[0, level, block],
            recv_sem=swap_sems.at[1, level, block],
            device_id={"depth": flip(level if level < levels else 0)},
            device_id_type=MESH,
        )

    def merge(level, block):
        swap(level, block).wait_recv()
        mine = part[block, side_bit] if level == 0 else comp[level - 1, block]
        theirs = got[level, block]
        front = lax.rem(position // (2**level), 2) == 0
        near_part = jnp.where(front, mine, theirs)
        far_part = jnp.where(front, theirs, mine)
        through = near_part[3]
        colour = [near_part[k] + through * far_part[k] for k in range(3)]
        through = through * far_part[3]
        if level == levels - 1:
            colour = [colour[k] + through * background[k] for k in range(3)]
            through = 1.0 - through
        for k in range(3):
            comp[level, block, k] = colour[k]
        comp[level, block, 3] = through
        swap(level + 1, block).start()

    inner = list(range(1, blocks - 1))
    outer = [0, blocks - 1]
    order = inner + outer
    passed_on = 0
    for n, block in enumerate(inner):
        render(block)
        swap(0, block).start()
        if n > 0:
            merge(0, inner[n - 1])
        if passed_on < halo_chunks - 1:
            pass_on(passed_on)
            passed_on += 1
    merge(0, inner[-1])

    for c in range(passed_on, halo_chunks):
        pass_on(c)

    for c in range(halo_chunks):

        @pl.when(gets_far)
        def _():
            far_copies[c].wait_recv()

        def fill_rim(g, _):
            near_rows = near[g].astype(jnp.float32)
            far_rows = far[g].astype(jnp.float32)
            above = jnp.where(is_odd, near_rows, far_rows)
            below = jnp.where(is_odd, far_rows, near_rows)
            for i in range(2):
                for t in range(col_tiles):
                    at = slice(t * LANES, (t + 1) * LANES)
                    rim = slice(i * RIM, (i + 1) * RIM)
                    ext[2 * g + i, t + 1, 0:RIM, :] = above[rim, at]
                    ext[2 * g + i, t + 1, RIM + rows : 2 * RIM + rows, :] = below[rim, at]
            return 0

        lax.fori_loop(c * per, (c + 1) * per, fill_rim, 0)
        render_rim(c)

    for level in range(1, levels):
        for block in inner:
            merge(level, block)
    for level in range(levels):
        for block in outer:
            merge(level, block)
    for block in order:
        swap(levels, block).wait_recv()
        at = pl.ds(block * RIM, RIM)
        mine = comp[levels - 1, block]
        theirs = got[levels, block]
        upper = side_bit == 1
        out[:, at, 0:half] = jnp.where(upper, theirs, mine)
        out[:, at, half:cols] = jnp.where(upper, mine, theirs)

    for c in range(halo_chunks):
        near_copies[c].wait_send()

        @pl.when(sends_on)
        def _():
            far_copies[c].wait_send()

    for level in range(levels + 1):
        for block in order:
            swap(level, block).wait_send()


def store(held, out, sem):
    copy = pltpu.make_async_copy(held, out, sem)
    copy.start()
    copy.wait()


def on_device(
    density, row_shift, brick_order, tf_gain, tf_bias, light_dir, background, *, n_depth, n_tile
):
    slices, rows, cols = density.shape
    levels = n_depth.bit_length() - 1
    blocks = rows // RIM
    halo_chunks = 4
    vmem = pl.BlockSpec(memory_space=pltpu.VMEM)
    halo = pltpu.VMEM((slices // 2, 2 * RIM, cols), density.dtype)
    image = (4, RIM, cols // 2)
    small_args = (row_shift, brick_order, tf_gain, tf_bias, light_dir, background)
    picture = pl.pallas_call(
        functools.partial(kernel, (n_depth, n_tile, halo_chunks)),
        out_shape=jax.ShapeDtypeStruct((4, rows, cols), jnp.float32),
        in_specs=[pl.BlockSpec(memory_space=pltpu.HBM)] * 7,
        out_specs=vmem,
        scratch_shapes=[
            *[pltpu.SMEM(arg.shape, arg.dtype) for arg in small_args],
            pltpu.VMEM(density.shape, density.dtype),
            pltpu.VMEM((4, cols // 2 // LANES, 5, RIM, LANES), jnp.float32),
            pltpu.VMEM((slices, cols // LANES + 2, rows + 2 * RIM, LANES), jnp.float32),
            halo,
            halo,
            halo,
            pltpu.VMEM((blocks, 2) + image, jnp.float32),
            pltpu.VMEM((levels + 1, blocks) + image, jnp.float32),
            pltpu.VMEM((levels, blocks) + image, jnp.float32),
            pltpu.SemaphoreType.DMA((3,)),
            pltpu.SemaphoreType.DMA((len(small_args),)),
            pltpu.SemaphoreType.DMA((4, halo_chunks)),
            pltpu.SemaphoreType.DMA((2, levels + 1, blocks)),
        ],
        compiler_params=pltpu.CompilerParams(
            collective_id=0, has_side_effects=True, vmem_limit_bytes=20 * 2**20
        ),
    )(*[pltpu.with_memory_space_constraint(arg, pltpu.HBM) for arg in (density, *small_args)])
    return pl.pallas_call(
        store,
        out_shape=jax.ShapeDtypeStruct((4, rows, cols), jnp.float32),
        in_specs=[vmem],
        out_specs=pl.BlockSpec(memory_space=pltpu.HBM),
        scratch_shapes=[pltpu.SemaphoreType.DMA],
        compiler_params=pltpu.CompilerParams(vmem_limit_bytes=2**20),
    )(picture)


def solution(mesh):
    placed = (P("depth", "tile", None), P("depth"), P(), P(), P(), P(), P())
    body = functools.partial(
        on_device, n_depth=mesh.shape["depth"], n_tile=mesh.shape["tile"]
    )
    return jax.shard_map(
        body, mesh=mesh, in_specs=placed, out_specs=P(None, "tile", None), check_vma=False
    )
```

```python
import functools
import math

import jax
import jax.numpy as jnp
from jax import lax
from jax.experimental import pallas as pl
from jax.experimental.pallas import tpu as pltpu
from jax.sharding import PartitionSpec as P

LANES = 128
RIM = 8
MESH = pl.DeviceIdType.MESH


def kernel(
    sizes,
    stored,
    row_shift_arg,
    brick_order_arg,
    gain_arg,
    bias_arg,
    light_arg,
    background_arg,
    out,
    row_shift,
    brick_order,
    gain,
    bias,
    light,
    background,
    density,
    state,
    ext,
    bundle,
    near,
    far,
    part,
    got,
    comp,
    load_sems,
    small_sems,
    halo_sems,
    swap_sems,
):
    n_depth, n_tile, halo_chunks = sizes
    slices, rows, cols = density.shape
    levels = n_depth.bit_length() - 1
    blocks = rows // RIM
    half = cols // 2
    half_tiles = half // LANES
    col_tiles = cols // LANES
    total = slices * n_depth
    me_d = lax.axis_index("depth")
    me_t = lax.axis_index("tile")
    odd = lax.rem(me_t, 2)
    pair_t = me_t + 1 - 2 * odd
    low_ok = me_t >= 2
    high_ok = me_t + 2 < n_tile
    is_odd = odd == 1
    sends_on = jnp.logical_or(
        jnp.logical_and(is_odd, low_ok), jnp.logical_and(jnp.logical_not(is_odd), high_ok)
    )
    gets_far = jnp.logical_or(
        jnp.logical_and(is_odd, high_ok), jnp.logical_and(jnp.logical_not(is_odd), low_ok)
    )
    on_t = me_t + 2 - 4 * odd

    def flip(level):
        bit = lax.rem(me_d // (2**level), 2)
        return me_d + (1 - 2 * bit) * 2**level

    loads = [
        pltpu.make_async_copy(
            stored.at[:, pl.ds(at, size)], density.at[:, pl.ds(at, size)], load_sems.at[i]
        )
        for i, (at, size) in enumerate(
            [(0, RIM), (rows - RIM, RIM), (RIM, rows - 2 * RIM)]
        )
    ]
    small = [
        pltpu.make_async_copy(arg, held, small_sems.at[i])
        for i, (arg, held) in enumerate(
            [
                (row_shift_arg, row_shift),
                (brick_order_arg, brick_order),
                (gain_arg, gain),
                (bias_arg, bias),
                (light_arg, light),
                (background_arg, background),
            ]
        )
    ]
    for load in small + loads:
        load.start()

    barrier = pltpu.get_barrier_semaphore()
    pl.semaphore_signal(barrier, inc=1, device_id={"tile": pair_t}, device_id_type=MESH)
    for level in range(levels):
        pl.semaphore_signal(barrier, inc=1, device_id={"depth": flip(level)}, device_id_type=MESH)

    @pl.when(low_ok)
    def _():
        pl.semaphore_signal(barrier, inc=1, device_id={"tile": me_t - 2}, device_id_type=MESH)

    @pl.when(high_ok)
    def _():
        pl.semaphore_signal(barrier, inc=1, device_id={"tile": me_t + 2}, device_id_type=MESH)

    place = lax.broadcasted_iota(jnp.int32, (RIM, cols), 0)

    def build(g, _):
        picked = []
        for i in range(2):
            j = 2 * g + i
            shift = row_shift[j]
            first = density[j, 0:RIM, :].astype(jnp.float32)
            last = density[j, rows - RIM : rows, :].astype(jnp.float32)
            use_last = jnp.where(shift > 0, 0, jnp.where(shift < 0, RIM, RIM // 2))
            picked.append(jnp.where(place >= use_last, last, first))
        bundle[g] = jnp.concatenate(picked, 0).astype(bundle.dtype)
        return 0

    for load in small + loads[:2]:
        load.wait()
    lax.fori_loop(0, slices // 2, build, 0)

    peers = 1 + levels + low_ok.astype(jnp.int32) + high_ok.astype(jnp.int32)
    pl.semaphore_wait(barrier, peers)

    quarter = slices // 2 // 4
    shift_size = quarter // 2
    starts = [0, quarter + shift_size, 2 * quarter + shift_size, 3 * quarter + shift_size]
    starts.append(slices // 2)
    near_copies = []
    far_copies = []
    for c in range(halo_chunks):
        span = pl.ds(starts[c], starts[c + 1] - starts[c])
        near_copies.append(
            pltpu.make_async_remote_copy(
                src_ref=bundle.at[span],
                dst_ref=near.at[span],
                send_sem=halo_sems.at[0, c],
                recv_sem=halo_sems.at[1, c],
                device_id={"tile": pair_t},
                device_id_type=MESH,
            )
        )
        far_copies.append(
            pltpu.make_async_remote_copy(
                src_ref=near.at[span],
                dst_ref=far.at[span],
                send_sem=halo_sems.at[2, c],
                recv_sem=halo_sems.at[3, c],
                device_id={"tile": on_t},
                device_id_type=MESH,
            )
        )
        near_copies[-1].start()

    @pl.when(jnp.logical_not(gets_far))
    def _():
        far[...] = jnp.zeros_like(far)

    loads[2].wait()

    def fill(j, _):
        sheet = density[j].astype(jnp.float32)
        ext[j, 0] = jnp.zeros((rows + 2 * RIM, LANES), jnp.float32)
        ext[j, col_tiles + 1] = jnp.zeros((rows + 2 * RIM, LANES), jnp.float32)
        for t in range(col_tiles):
            ext[j, t + 1, RIM : RIM + rows, :] = sheet[:, t * LANES : (t + 1) * LANES]
        return 0

    lax.fori_loop(0, slices, fill, 0)

    def pass_on(c):
        near_copies[c].wait_recv()

        @pl.when(sends_on)
        def _():
            far_copies[c].start()

    lane = lax.broadcasted_iota(jnp.int32, (RIM, LANES), 1)
    is_first = lane == 0
    is_last = lane == LANES - 1
    log2e = math.log2(math.e)
    half_gain = [0.5 * gain[k] for k in range(3)]
    half_bias = [0.5 * bias[k] for k in range(3)]
    opt_gain = gain[3] * log2e
    opt_bias = bias[3] * log2e
    light_c = 0.5 * light[0]
    light_r = 0.5 * light[1]
    light_z = light[2]

    def advance(block, side, low, high, carry):
        def step(j, carry):
            base = RIM + block * RIM - 1 - row_shift[j]
            first_tile = side * half_tiles
            value = [ext[j, first_tile + i, pl.ds(base + 1, RIM), :] for i in range(half_tiles + 2)]
            new = []
            for i in range(half_tiles):
                t = first_tile + i + 1
                through, base_sum, c0, c1, c2 = carry[i]
                v = value[i + 1]
                above = ext[j, t, pl.ds(base, RIM), :]
                below = ext[j, t, pl.ds(base + 2, RIM), :]
                left = pltpu.roll(jnp.where(is_last, value[i], v), 1, 1)
                right = pltpu.roll(jnp.where(is_first, value[i + 2], v), LANES - 1, 1)
                drow = below - above
                dcol = right - left
                norm = lax.rsqrt(4.0 + (dcol * dcol + drow * drow))
                shade = 0.125 + jnp.abs(light_z - light_c * dcol - light_r * drow) * norm
                grow = jnp.exp2(opt_gain * v + opt_bias)
                passed = jnp.exp2(jnp.log(1.0 + grow) * (-log2e / total))
                after = through * passed
                weight = (through - after) * shade
                sums = [
                    c + weight * jnp.tanh(half_gain[k] * v + half_bias[k])
                    for k, c in enumerate((c0, c1, c2))
                ]
                new.append((after, base_sum + weight, *sums))
            return tuple(new)

        return lax.fori_loop(low, high, step, carry, unroll=next(u for u in (4, 3, 2, 1) if (high - low) % u == 0))

    def finish(block, side, carry):
        for i in range(half_tiles):
            through, base_sum, *sums = carry[i]
            at = slice(i * LANES, (i + 1) * LANES)
            for k in range(3):
                part[block, side, k, :, at] = base_sum + sums[k]
            part[block, side, 3, :, at] = through

    zero = jnp.zeros((RIM, LANES), jnp.float32)
    one = jnp.ones((RIM, LANES), jnp.float32)
    start = tuple((one, zero, zero, zero, zero) for _ in range(half_tiles))

    def render(block):
        def one_side(side, _):
            finish(block, side, advance(block, side, 0, slices, start))
            return 0

        lax.fori_loop(0, 2, one_side, 0)

    def render_rim(c):
        def one_piece(piece, block):
            side = lax.rem(piece, 2)
            if c == 0:
                carry = start
            else:
                carry = tuple(
                    tuple(state[piece, i, k] for k in range(5)) for i in range(half_tiles)
                )
            carry = advance(block, side, 2 * starts[c], 2 * starts[c + 1], carry)
            if c == halo_chunks - 1:
                finish(block, side, carry)
            else:
                for i in range(half_tiles):
                    for k in range(5):
                        state[piece, i, k] = carry[i][k]
            return block

        for rim, block in enumerate(outer):
            lax.fori_loop(2 * rim, 2 * rim + 2, one_piece, block)
            if c == halo_chunks - 1:
                swap(0, block).start()

    side_bit = lax.rem(me_d, 2)
    position = brick_order[me_d]

    def swap(level, block):
        if level == 0:
            source = part.at[block, 1 - side_bit]
        else:
            source = comp.at[level - 1, block]
        return pltpu.make_async_remote_copy(
            src_ref=source,
            dst_ref=got.at[level, block],
            send_sem=swap_sems.at[0, level, block],
            recv_sem=swap_sems.at[1, level, block],
            device_id={"depth": flip(level if level < levels else 0)},
            device_id_type=MESH,
        )

    def merge(level, block):
        swap(level, block).wait_recv()
        mine = part[block, side_bit] if level == 0 else comp[level - 1, block]
        theirs = got[level, block]
        front = lax.rem(position // (2**level), 2) == 0
        near_part = jnp.where(front, mine, theirs)
        far_part = jnp.where(front, theirs, mine)
        through = near_part[3]
        colour = [near_part[k] + through * far_part[k] for k in range(3)]
        through = through * far_part[3]
        if level == levels - 1:
            colour = [colour[k] + through * background[k] for k in range(3)]
            through = 1.0 - through
        for k in range(3):
            comp[level, block, k] = colour[k]
        comp[level, block, 3] = through
        swap(level + 1, block).start()

    inner = list(range(1, blocks - 1))
    outer = [0, blocks - 1]
    order = inner + outer
    passed_on = 0
    for n, block in enumerate(inner):
        render(block)
        swap(0, block).start()
        if n > 0:
            merge(0, inner[n - 1])
        if passed_on < halo_chunks - 1:
            pass_on(passed_on)
            passed_on += 1
    merge(0, inner[-1])

    for c in range(passed_on, halo_chunks):
        pass_on(c)

    for c in range(halo_chunks):

        @pl.when(gets_far)
        def _():
            far_copies[c].wait_recv()

        def fill_rim(g, _):
            near_rows = near[g].astype(jnp.float32)
            far_rows = far[g].astype(jnp.float32)
            above = jnp.where(is_odd, near_rows, far_rows)
            below = jnp.where(is_odd, far_rows, near_rows)
            for i in range(2):
                for t in range(col_tiles):
                    at = slice(t * LANES, (t + 1) * LANES)
                    rim = slice(i * RIM, (i + 1) * RIM)
                    ext[2 * g + i, t + 1, 0:RIM, :] = above[rim, at]
                    ext[2 * g + i, t + 1, RIM + rows : 2 * RIM + rows, :] = below[rim, at]
            return 0

        lax.fori_loop(starts[c], starts[c + 1], fill_rim, 0)
        render_rim(c)

    for level in range(1, levels):
        for block in inner:
            merge(level, block)
    for level in range(levels):
        for block in outer:
            merge(level, block)
    for block in order:
        swap(levels, block).wait_recv()
        at = pl.ds(block * RIM, RIM)
        mine = comp[levels - 1, block]
        theirs = got[levels, block]
        upper = side_bit == 1
        out[:, at, 0:half] = jnp.where(upper, theirs, mine)
        out[:, at, half:cols] = jnp.where(upper, mine, theirs)

    for c in range(halo_chunks):
        near_copies[c].wait_send()

        @pl.when(sends_on)
        def _():
            far_copies[c].wait_send()

    for level in range(levels + 1):
        for block in order:
            swap(level, block).wait_send()


def store(held, out, sem):
    copy = pltpu.make_async_copy(held, out, sem)
    copy.start()
    copy.wait()


def on_device(
    density, row_shift, brick_order, tf_gain, tf_bias, light_dir, background, *, n_depth, n_tile
):
    slices, rows, cols = density.shape
    levels = n_depth.bit_length() - 1
    blocks = rows // RIM
    halo_chunks = 4
    vmem = pl.BlockSpec(memory_space=pltpu.VMEM)
    halo = pltpu.VMEM((slices // 2, 2 * RIM, cols), density.dtype)
    image = (4, RIM, cols // 2)
    small_args = (row_shift, brick_order, tf_gain, tf_bias, light_dir, background)
    picture = pl.pallas_call(
        functools.partial(kernel, (n_depth, n_tile, halo_chunks)),
        out_shape=jax.ShapeDtypeStruct((4, rows, cols), jnp.float32),
        in_specs=[pl.BlockSpec(memory_space=pltpu.HBM)] * 7,
        out_specs=vmem,
        scratch_shapes=[
            *[pltpu.SMEM(arg.shape, arg.dtype) for arg in small_args],
            pltpu.VMEM(density.shape, density.dtype),
            pltpu.VMEM((4, cols // 2 // LANES, 5, RIM, LANES), jnp.float32),
            pltpu.VMEM((slices, cols // LANES + 2, rows + 2 * RIM, LANES), jnp.float32),
            halo,
            halo,
            halo,
            pltpu.VMEM((blocks, 2) + image, jnp.float32),
            pltpu.VMEM((levels + 1, blocks) + image, jnp.float32),
            pltpu.VMEM((levels, blocks) + image, jnp.float32),
            pltpu.SemaphoreType.DMA((3,)),
            pltpu.SemaphoreType.DMA((len(small_args),)),
            pltpu.SemaphoreType.DMA((4, halo_chunks)),
            pltpu.SemaphoreType.DMA((2, levels + 1, blocks)),
        ],
        compiler_params=pltpu.CompilerParams(
            collective_id=0, has_side_effects=True, vmem_limit_bytes=20 * 2**20
        ),
    )(*[pltpu.with_memory_space_constraint(arg, pltpu.HBM) for arg in (density, *small_args)])
    return pl.pallas_call(
        store,
        out_shape=jax.ShapeDtypeStruct((4, rows, cols), jnp.float32),
        in_specs=[vmem],
        out_specs=pl.BlockSpec(memory_space=pltpu.HBM),
        scratch_shapes=[pltpu.SemaphoreType.DMA],
        compiler_params=pltpu.CompilerParams(vmem_limit_bytes=2**20),
    )(picture)


def solution(mesh):
    placed = (P("depth", "tile", None), P("depth"), P(), P(), P(), P(), P())
    body = functools.partial(
        on_device, n_depth=mesh.shape["depth"], n_tile=mesh.shape["tile"]
    )
    return jax.shard_map(
        body, mesh=mesh, in_specs=placed, out_specs=P(None, "tile", None), check_vma=False
    )
```
